256 devices in a mesh: row: 32 (over z_lo, y, core), col: 8 (over z_hi, x).
Axes of the slice: x: 4, y: 4, z: 8 (z_hi: 2, z_lo: 4; z = z_hi * 4 + z_lo), core: 2. Of those that a mesh axis runs over, the one named last changes fastest.
Arguments:
- slab: bfloat16 [32768, 16384], P('row', 'col'), may hold values from -6 to 6
- panel_left: bfloat16 [32768, 512], P('row', 'col'), may hold values from -3 to 3
- panel_top: bfloat16 [512, 16384], P('row', 'col'), may hold values from -3 to 3
- row_bases: bfloat16 [32768, 256], P('row'), may hold values from -0.25 to 0.25
- col_bases: bfloat16 [16384, 256], P('col'), may hold values from -0.25 to 0.25
- row_ranks: int32 [64], P('row'), may hold values from 32 to 256, as said below
- col_ranks: int32 [32], P('col'), may hold values from 32 to 256, as said below
- pivot_inverse: bfloat16 [512, 512], replicated, may hold values from -0.0625 to 0.0625
- pivot_rhs: bfloat16 [512, 4096], P('row', 'col'), may hold values from -6 to 6
- rhs: bfloat16 [32768, 4096], P('row', 'col'), may hold values from -6 to 6
Outputs:
- slab_new: bfloat16 [32768, 16384], P('row', 'col')
- rhs_new: bfloat16 [32768, 4096], P('row', 'col')
The draws below stay inside these ranges and needn't reach their ends.
Inputs may be any that keep to these rules, and one draw needn't show every extreme that they name: `row_ranks`: each entry is the rank of one tile; the value 256 occurs in every draw. `col_ranks`: each entry is the rank of one tile; the value 256 occurs in every draw.
All inputs are finite; a program needn't handle non-finite values.
Results may differ from the reference program's by a relative error of at most 0.0062.
Values may be sent and summed in bfloat16 or wider, within the bound.
No kernel may reach another device: no remote copies, remote signals or barrier semaphores. Data moves between devices by JAX's collectives and lax.ppermute only.
A program may use at most 128 MiB of HBM per device.

```python
import jax
import jax.numpy as jnp
from jax import lax

B = 512
RMAX = 256
LOW_RANK = 32
ROW_TILES = 64
COL_TILES = 32
ROWS = 32768
COLS = 16384
GAINS = 4096


def spread_ranks(key, count):
    first_key, second_key = jax.random.split(jax.random.fold_in(key, 17))
    values = jax.random.randint(first_key, (count,), LOW_RANK, RMAX + 1).astype(jnp.int32)
    where = jax.random.randint(second_key, (), 0, count).astype(jnp.int32)
    values = values.at[where].set(RMAX)
    return values


def draw_row_ranks(key, part):
    return spread_ranks(jax.random.fold_in(key, 101), ROW_TILES)


def draw_col_ranks(key, part):
    return spread_ranks(jax.random.fold_in(key, 202), COL_TILES)


def block_scale(rng, shape, pieces, least, top_value):
    level = 1.0
    for position, parts in pieces:
        draws = jax.random.uniform(jax.random.fold_in(jax.random.fold_in(rng, 6), position), (parts,), jnp.float32, least / len(pieces), top_value / len(pieces))
        level = level * jnp.repeat(jnp.exp(draws), shape[position] // parts).reshape((-1,) + (1,) * (len(shape) - 1 - position))
    return level


def gaussian(key, shape, scale, bound, shards=(), kind=jnp.bfloat16):
    level = block_scale(key, shape, shards, -0.22, 0.18) if shards else 1.0
    array = jax.random.normal(key, shape, jnp.float32) * scale * level
    return jnp.minimum(jnp.maximum(array, -bound), bound).astype(kind)


def setup_inputs(seed: int = 0) -> dict:
    key_list = jax.random.split(jax.random.key(seed), 11)
    return {
        "slab": gaussian(key_list[0], (ROWS, COLS), 1.0, 6.0, ((0, 32), (1, 8))),
        "panel_left": gaussian(key_list[1], (ROWS, B), 0.4, 3.0, ((0, 32), (1, 8))),
        "panel_top": gaussian(key_list[2], (B, COLS), 0.4, 3.0, ((0, 32), (1, 8))),
        "row_bases": gaussian(key_list[3], (ROWS, RMAX), B ** -0.5, 0.25, ((0, 32),)),
        "col_bases": gaussian(key_list[4], (COLS, RMAX), B ** -0.5, 0.25, ((0, 8),)),
        "row_ranks": draw_row_ranks(jax.random.fold_in(key_list[10], 71), 0),
        "col_ranks": draw_col_ranks(jax.random.fold_in(key_list[10], 71), 0),
        "pivot_inverse": gaussian(key_list[7], (B, B), (16 * B) ** -0.5, 0.0625),
        "pivot_rhs": gaussian(key_list[8], (B, GAINS), 1.0, 6.0, ((0, 32), (1, 8))),
        "rhs": gaussian(key_list[9], (ROWS, GAINS), 1.0, 6.0, ((0, 32), (1, 8))),
    }


def reference(slab, panel_left, panel_top, row_bases, col_bases, row_ranks, col_ranks, pivot_inverse, pivot_rhs, rhs):
    levels = jnp.arange(RMAX, dtype=jnp.int32)
    keep_row = (levels[None, :] < row_ranks[:, None]).astype(jnp.float32)
    keep_column = (levels[None, :] < col_ranks[:, None]).astype(jnp.float32)
    left_bases = row_bases.reshape(ROW_TILES, B, RMAX).astype(jnp.float32)
    right_bases = col_bases.reshape(COL_TILES, B, RMAX).astype(jnp.float32)
    left_tiles = panel_left.reshape(ROW_TILES, B, B).astype(jnp.float32)
    row_core = (jnp.einsum("tbr,tbc->trc", left_bases, left_tiles) * keep_row[:, :, None]).astype(jnp.bfloat16)
    upper_rows = panel_top.reshape(B, COL_TILES, B).astype(jnp.float32)
    column_core = (jnp.einsum("pjc,jcr->pjr", upper_rows, right_bases) * keep_column[None]).astype(jnp.bfloat16)
    column_wide = column_core.astype(jnp.float32)
    slab_tiles = slab.reshape(ROW_TILES, B, COLS)

    def one_row(packed):
        core_rows, basis, block = packed
        core_block = jnp.einsum("rp,pjs->jrs", core_rows.astype(jnp.float32), column_wide).astype(jnp.bfloat16)
        spread = jnp.einsum("br,jrs->jbs", basis, core_block.astype(jnp.float32)).astype(jnp.bfloat16)
        change = jnp.einsum("jbs,jcs->bjc", spread.astype(jnp.float32), right_bases).reshape(B, COLS)
        return (block.astype(jnp.float32) - change).astype(jnp.bfloat16)

    slab_new = lax.map(one_row, (row_core, left_bases, slab_tiles)).reshape(ROWS, COLS)
    pivot_solution = jnp.dot(pivot_inverse, pivot_rhs, preferred_element_type=jnp.float32).astype(jnp.bfloat16)
    reduced = jnp.einsum("irp,pg->irg", row_core.astype(jnp.float32), pivot_solution.astype(jnp.float32)).astype(jnp.bfloat16)
    lowered = jnp.einsum("ibr,irg->ibg", left_bases, reduced.astype(jnp.float32)).reshape(ROWS, GAINS)
    rhs_new = (rhs.astype(jnp.float32) - lowered).astype(jnp.bfloat16)
    return slab_new, rhs_new
```

```python
import jax
import jax.numpy as jnp
from jax import lax
from jax.experimental import pallas as pl
from jax.experimental.pallas import tpu as pltpu
from jax.sharding import PartitionSpec as P


ROW, COL = 32, 8
BF = jnp.bfloat16
F32 = jnp.float32
VMEM = pl.BlockSpec(memory_space=pltpu.VMEM)
SMEM = pl.BlockSpec(memory_space=pltpu.SMEM)
ANY = pl.BlockSpec(memory_space=pl.ANY)
HBM = pl.BlockSpec(memory_space=pltpu.HBM)


def dot(a, b):
    return lax.dot_general(a, b, (((1,), (0,)), ((), ())), preferred_element_type=F32)


def dot_t(a, b):
    return lax.dot_general(a, b, (((1,), (1,)), ((), ())), preferred_element_type=F32)


def exchange(array, zl=0, y=0, core=0, zh=0, x=0):
    row_bits = zl * 8 + y * 2 + core
    col_bits = zh * 4 + x
    pairs = [
        (r * COL + c, (r ^ row_bits) * COL + (c ^ col_bits)) for r in range(ROW) for c in range(COL)
    ]
    return lax.ppermute(array, ("row", "col"), pairs)


def grant(mib):
    return pltpu.CompilerParams(vmem_limit_bytes=mib << 20)


def cost(flops, bytes_accessed):
    return pl.CostEstimate(flops=flops, bytes_accessed=bytes_accessed, transcendentals=0)


def project_kernel(
    row_ranks_h, col_ranks_h, left_t, bases, top, right, pivot,
    kt_ref, pack_ref, lt_v, bases_v, top_v, right_v, row_ranks, col_ranks, sems,
):
    tile = 512
    sources = [(top, top_v), (left_t, lt_v), (pivot, pack_ref.at[:, 1024:])]
    sources += [(right.at[j * tile : (j + 1) * tile], right_v.at[j * tile : (j + 1) * tile]) for j in range(4)]
    sources += [(bases.at[i * tile : (i + 1) * tile], bases_v.at[i * tile : (i + 1) * tile]) for i in range(2)]
    sources += [(col_ranks_h, col_ranks), (row_ranks_h, row_ranks)]
    copies = [pltpu.make_async_copy(a, b, sems.at[n]) for n, (a, b) in enumerate(sources)]
    for copy in copies:
        copy.start()
    copies[9].wait()
    copies[10].wait()
    lane = lax.broadcasted_iota(jnp.int32, (16, 256), 1)
    copies[0].wait()
    for j in range(4):
        copies[3 + j].wait()
        part = dot(top_v[:, j * tile : (j + 1) * tile], right_v[j * tile : (j + 1) * tile, :])
        part = jnp.where(lane < col_ranks[j], part, 0.0)
        pack_ref[:, j * 256 : (j + 1) * 256] = part.astype(BF)
    lane = lax.broadcasted_iota(jnp.int32, (64, 256), 1)
    copies[1].wait()
    for i in range(2):
        copies[7 + i].wait()
        part = dot(lt_v[:, i * tile : (i + 1) * tile], bases_v[i * tile : (i + 1) * tile, :])
        part = jnp.where(lane < row_ranks[i], part, 0.0)
        kt_ref[:, i * 256 : (i + 1) * 256] = part.astype(BF)
    copies[2].wait()


def project(row_ranks, col_ranks, left_t, bases, top, right, pivot):
    return pl.pallas_call(
        project_kernel,
        out_shape=(
            jax.ShapeDtypeStruct((64, 512), BF),
            jax.ShapeDtypeStruct((16, 1536), BF),
        ),
        in_specs=[HBM] * 7,
        out_specs=(VMEM, VMEM),
        scratch_shapes=[
            pltpu.VMEM((64, 1024), BF),
            pltpu.VMEM((1024, 256), BF),
            pltpu.VMEM((16, 2048), BF),
            pltpu.VMEM((2048, 256), BF),
            pltpu.SMEM((2,), jnp.int32),
            pltpu.SMEM((4,), jnp.int32),
            pltpu.SemaphoreType.DMA((11,)),
        ],
        compiler_params=grant(8),
        cost_estimate=cost(50_000_000, 1_800_000),
        name="project",
    )(*(in_hbm(a) for a in (row_ranks, col_ranks, left_t, bases, top, right, pivot)))


def in_hbm(array):
    return pltpu.with_memory_space_constraint(array, pltpu.HBM)


def load_kernel(after, *refs):
    del after
    count = (len(refs) - 1) // 2
    sems = refs[-1]
    copies = [pltpu.make_async_copy(refs[n], refs[count + n], sems.at[n]) for n in range(count)]
    for copy in copies:
        copy.start()
    for copy in copies:
        copy.wait()


def load(after, *arrays):
    return pl.pallas_call(
        load_kernel,
        out_shape=tuple(jax.ShapeDtypeStruct(a.shape, a.dtype) for a in arrays),
        in_specs=[ANY] + [HBM] * len(arrays),
        out_specs=(VMEM,) * len(arrays),
        scratch_shapes=[pltpu.SemaphoreType.DMA((len(arrays),))],
        compiler_params=grant(10),
        cost_estimate=cost(0, 14_000_000),
        name="load",
    )(after, *(in_hbm(a) for a in arrays))


def join_kernel(p0, p1, p2, p3, k0, k1, m_ref, k_ref):
    for n, piece in enumerate((p0, p1, p2, p3)):
        m_ref[n * 16 : (n + 1) * 16, :] = piece[...]
    k_ref[:64, :] = k0[...]
    k_ref[64:, :] = k1[...]


def join(packs, parts):
    return pl.pallas_call(
        join_kernel,
        out_shape=(
            jax.ShapeDtypeStruct((64, 1536), BF),
            jax.ShapeDtypeStruct((128, 512), BF),
        ),
        in_specs=[VMEM] * 6,
        out_specs=(VMEM,) * 2,
        compiler_params=grant(6),
        cost_estimate=cost(0, 700_000),
        name="join",
    )(*packs, *parts)


def place():
    r = lax.axis_index("row")
    c = lax.axis_index("col")
    return r // 8, (r // 2) % 4, r % 2, c // 4, c % 4


def blocks():
    zl, y, core, zh, x = place()
    n = 0
    for half in range(2):
        for dy in range(4):
            for dz in range(4):
                z_from, y_from, core_from = zl ^ dz, y ^ dy, core ^ half
                natural = (z_from * 4 + y_from) * 32 + core_from * 16
                col_from = z_from * 2 + y_from // 2
                stacked = (
                    ((col_from % 4) ^ x) * 128
                    + ((col_from // 4) ^ zh) * 64
                    + (y_from % 2) * 32
                    + core_from * 16
                )
                yield n * 16, pl.multiple_of(natural, 16), pl.multiple_of(stacked, 16)
                n += 1


def left_kernel(k0, k1, k2, k3, bases, g_ref, stack, ordered):
    for n, piece in enumerate((k0, k1, k2, k3)):
        stack[n * 128 : (n + 1) * 128, :] = piece[...]
    for at, _, stacked in blocks():
        ordered[at : at + 16, :] = stack[pl.ds(stacked, 16), :]
    for i in range(2):
        rows = slice(i * 512, (i + 1) * 512)
        g_ref[rows, :] = dot_t(bases[rows, :], ordered[:, i * 256 : (i + 1) * 256]).astype(BF)


def left_product(parts, bases):
    return pl.pallas_call(
        left_kernel,
        out_shape=jax.ShapeDtypeStruct((1024, 512), BF),
        in_specs=[VMEM] * 5,
        out_specs=VMEM,
        scratch_shapes=[pltpu.VMEM((512, 512), BF), pltpu.VMEM((512, 512), BF)],
        cost_estimate=cost(270_000_000, 2_000_000),
        compiler_params=grant(10),
        name="left_product",
    )(*parts, bases)


def update_kernel(g, p0, p1, p2, p3, p4, p5, p6, p7, right, slab, rhs, inverse, slab_out, rhs_out, wide, slab_v, rhs_v, natural, solved, ordered, sems):
    pieces = (p0, p1, p2, p3, p4, p5, p6, p7)
    tile = 512
    for j in range(4):
        core = jnp.concatenate([p[:, j * 256 : (j + 1) * 256] for p in pieces], axis=0)
        for i in range(2):
            rows = slice(i * tile, (i + 1) * tile)
            wide[j, rows, :] = dot(g[rows, :], core).astype(BF)
    copies = []
    for j in range(4):
        cols = slice(j * tile, (j + 1) * tile)
        change = dot_t(wide[j], right[cols, :])
        slab_v[:, cols] = (slab[:, cols].astype(F32) - change).astype(BF)
        copies.append(pltpu.make_async_copy(slab_v.at[:, cols], slab_out.at[:, cols], sems.at[j]))
        copies[-1].start()
    for at, to, _ in blocks():
        natural[pl.ds(to, 16), :] = pieces[at // 64][at % 64 : at % 64 + 16, 1024:]
    solved[...] = dot(inverse[...], natural[...]).astype(BF)
    for at, to, _ in blocks():
        ordered[at : at + 16, :] = solved[pl.ds(to, 16), :]
    for i in range(2):
        rows = slice(i * tile, (i + 1) * tile)
        rhs_v[rows, :] = (rhs[rows, :].astype(F32) - dot(g[rows, :], ordered[...])).astype(BF)
        copies.append(pltpu.make_async_copy(rhs_v.at[rows], rhs_out.at[rows], sems.at[4 + i]))
        copies[-1].start()
    for copy in copies:
        copy.wait()


def update(g, pieces, right, slab, rhs, inverse):
    return pl.pallas_call(
        update_kernel,
        out_shape=(
            jax.ShapeDtypeStruct((1024, 2048), BF),
            jax.ShapeDtypeStruct((1024, 512), BF),
        ),
        in_specs=[VMEM] * 13,
        out_specs=(HBM, HBM),
        scratch_shapes=[
            pltpu.VMEM((4, 1024, 256), BF),
            pltpu.VMEM((1024, 2048), BF),
            pltpu.VMEM((1024, 512), BF),
            pltpu.VMEM((512, 512), BF),
            pltpu.VMEM((512, 512), BF),
            pltpu.VMEM((512, 512), BF),
            pltpu.SemaphoreType.DMA((6,)),
        ],
        compiler_params=grant(28),
        cost_estimate=cost(3_000_000_000, 16_000_000),
        name="update",
    )(g, *pieces, right, slab, rhs, inverse)


def per_device(
    slab,
    panel_left,
    panel_top,
    row_bases,
    col_bases,
    row_ranks,
    col_ranks,
    pivot_inverse,
    pivot_rhs,
    rhs,
):
    part, pack = project(
        row_ranks, col_ranks, panel_left.T, row_bases, panel_top, col_bases, pivot_rhs
    )
    part_far = exchange(part, zh=1)
    packs = [pack] + [exchange(pack, zl=d) for d in (1, 2, 3)]
    bases, right, slab, rhs, inverse = load(
        pack, row_bases, col_bases, slab, rhs, pivot_inverse
    )
    piece, left_part = join(packs, (part, part_far))
    pieces = [piece] + [exchange(piece, y=d) for d in (1, 2, 3)]
    lefts = [left_part] + [exchange(left_part, x=d) for d in (1, 2, 3)]
    pieces += [exchange(p, core=1) for p in pieces]
    g = left_product(lefts, bases)
    return update(g, pieces, right, slab, rhs, inverse)


def solution(mesh):
    in_specs = (
        P("row", "col"),
        P("row", "col"),
        P("row", "col"),
        P("row", None),
        P("col", None),
        P("row"),
        P("col"),
        P(),
        P("row", "col"),
        P("row", "col"),
    )
    out_specs = (P("row", "col"), P("row", "col"))
    return jax.shard_map(
        per_device, mesh=mesh, in_specs=in_specs, out_specs=out_specs, check_vma=False
    )
```

```python
import jax
import jax.numpy as jnp
from jax import lax
from jax.experimental import pallas as pl
from jax.experimental.pallas import tpu as pltpu
from jax.sharding import PartitionSpec as P


ROW, COL = 32, 8
BF = jnp.bfloat16
F32 = jnp.float32
VMEM = pl.BlockSpec(memory_space=pltpu.VMEM)
SMEM = pl.BlockSpec(memory_space=pltpu.SMEM)
ANY = pl.BlockSpec(memory_space=pl.ANY)
HBM = pl.BlockSpec(memory_space=pltpu.HBM)


def dot(a, b):
    return lax.dot_general(a, b, (((1,), (0,)), ((), ())), preferred_element_type=F32)


def dot_t(a, b):
    return lax.dot_general(a, b, (((1,), (1,)), ((), ())), preferred_element_type=F32)


def exchange(array, zl=0, y=0, core=0, zh=0, x=0):
    row_bits = zl * 8 + y * 2 + core
    col_bits = zh * 4 + x
    pairs = [
        (r * COL + c, (r ^ row_bits) * COL + (c ^ col_bits)) for r in range(ROW) for c in range(COL)
    ]
    return lax.ppermute(array, ("row", "col"), pairs)


def grant(mib):
    return pltpu.CompilerParams(vmem_limit_bytes=mib << 20)


def cost(flops, bytes_accessed):
    return pl.CostEstimate(flops=flops, bytes_accessed=bytes_accessed, transcendentals=0)


def in_hbm(array):
    return pltpu.with_memory_space_constraint(array, pltpu.HBM)


def start_all(sources, sems):
    copies = [pltpu.make_async_copy(a, b, sems.at[n]) for n, (a, b) in enumerate(sources)]
    for copy in copies:
        copy.start()
    return copies


def project_kernel(ranks_h, rows_h, left_h, bases_h, top_h, right_h, pivot_h,
                   pack, kt, bases, right, left, top, row_ranks, ranks, sems):
    tile = 512
    sources = [(top_h, top), (ranks_h, ranks), (rows_h, row_ranks)]
    for j in range(4):
        part = slice(j * tile, (j + 1) * tile)
        sources.append((right_h.at[part], right.at[part]))
    sources.append((left_h, left))
    for i in range(2):
        part = slice(i * tile, (i + 1) * tile)
        sources.append((bases_h.at[part], bases.at[part]))
    sources.append((pivot_h, pack.at[:, 1024:]))
    copies = start_all(sources, sems)
    lane = lax.broadcasted_iota(jnp.int32, (16, 256), 1)
    for copy in copies[:3]:
        copy.wait()
    for j in range(4):
        copies[3 + j].wait()
        part = dot(top[:, j * tile : (j + 1) * tile], right[j * tile : (j + 1) * tile, :])
        part = jnp.where(lane < ranks[j], part, 0.0)
        pack[:, j * 256 : (j + 1) * 256] = part.astype(BF)
    lane = lax.broadcasted_iota(jnp.int32, (64, 256), 1)
    copies[7].wait()
    for i in range(2):
        copies[8 + i].wait()
        part = dot(left[:, i * tile : (i + 1) * tile], bases[i * tile : (i + 1) * tile, :])
        part = jnp.where(lane < row_ranks[i], part, 0.0)
        kt[:, i * 256 : (i + 1) * 256] = part.astype(BF)
    copies[10].wait()


def project(ranks, row_ranks, left_t, bases, top, right, pivot):
    return pl.pallas_call(
        project_kernel,
        out_shape=(
            jax.ShapeDtypeStruct((16, 1536), BF),
            jax.ShapeDtypeStruct((64, 512), BF),
            jax.ShapeDtypeStruct((1024, 256), BF),
            jax.ShapeDtypeStruct((2048, 256), BF),
        ),
        in_specs=[HBM] * 7,
        out_specs=(VMEM,) * 4,
        scratch_shapes=[
            pltpu.VMEM((64, 1024), BF),
            pltpu.VMEM((16, 2048), BF),
            pltpu.SMEM((2,), jnp.int32),
            pltpu.SMEM((4,), jnp.int32),
            pltpu.SemaphoreType.DMA((11,)),
        ],
        compiler_params=grant(8),
        cost_estimate=cost(50_000_000, 1_800_000),
        name="project",
    )(*(in_hbm(a) for a in (ranks, row_ranks, left_t, bases, top, right, pivot)))


def load_kernel(*refs):
    count = (len(refs) - 1) // 2
    copies = start_all(list(zip(refs[:count], refs[count:-1])), refs[-1])
    for copy in copies:
        copy.wait()


def load(*arrays):
    return pl.pallas_call(
        load_kernel,
        out_shape=[jax.ShapeDtypeStruct(a.shape, a.dtype) for a in arrays],
        in_specs=[HBM] * len(arrays),
        out_specs=[VMEM] * len(arrays),
        scratch_shapes=[pltpu.SemaphoreType.DMA((len(arrays),))],
        compiler_params=grant(10),
        cost_estimate=cost(0, 8_000_000),
    )(*(in_hbm(a) for a in arrays))


def join_kernel(*refs):
    out = refs[-1]
    rows = refs[0].shape[0]
    for n, piece in enumerate(refs[:-1]):
        out[n * rows : (n + 1) * rows, :] = piece[...]


def join(pieces):
    rows, columns = pieces[0].shape
    return pl.pallas_call(
        join_kernel,
        out_shape=jax.ShapeDtypeStruct((len(pieces) * rows, columns), BF),
        in_specs=[VMEM] * len(pieces),
        out_specs=VMEM,
        compiler_params=grant(4),
        cost_estimate=cost(0, 300_000),
    )(*pieces)


def place():
    r = lax.axis_index("row")
    c = lax.axis_index("col")
    return r // 8, (r // 2) % 4, r % 2, c // 4, c % 4


def blocks():
    zl, y, core, zh, x = place()
    n = 0
    for half in range(2):
        for dy in range(4):
            for dz in range(4):
                z_from, y_from, core_from = zl ^ dz, y ^ dy, core ^ half
                natural = (z_from * 4 + y_from) * 32 + core_from * 16
                col_from = z_from * 2 + y_from // 2
                stacked = (
                    ((col_from % 4) ^ x) * 128
                    + ((col_from // 4) ^ zh) * 64
                    + (y_from % 2) * 32
                    + core_from * 16
                )
                yield n * 16, pl.multiple_of(natural, 16), pl.multiple_of(stacked, 16)
                n += 1


def left_kernel(k0, k1, k2, k3, bases, g_ref, stack, ordered):
    for n, piece in enumerate((k0, k1, k2, k3)):
        stack[n * 128 : (n + 1) * 128, :] = piece[...]
    for at, _, stacked in blocks():
        ordered[at : at + 16, :] = stack[pl.ds(stacked, 16), :]
    for i in range(2):
        rows = slice(i * 512, (i + 1) * 512)
        g_ref[rows, :] = dot_t(bases[rows, :], ordered[:, i * 256 : (i + 1) * 256]).astype(BF)


def left_product(parts, bases):
    return pl.pallas_call(
        left_kernel,
        out_shape=jax.ShapeDtypeStruct((1024, 512), BF),
        in_specs=[VMEM] * 5,
        out_specs=VMEM,
        scratch_shapes=[pltpu.VMEM((512, 512), BF), pltpu.VMEM((512, 512), BF)],
        cost_estimate=cost(270_000_000, 2_000_000),
        compiler_params=grant(10),
        name="left_product",
    )(*parts, bases)


def solve_kernel(p0, p1, p2, p3, p4, p5, p6, p7, inverse, ordered, natural, solved):
    pieces = (p0, p1, p2, p3, p4, p5, p6, p7)
    for at, to, _ in blocks():
        natural[pl.ds(to, 16), :] = pieces[at // 64][at % 64 : at % 64 + 16, 1024:]
    solved[...] = dot(inverse[...], natural[...]).astype(BF)
    for at, to, _ in blocks():
        ordered[at : at + 16, :] = solved[pl.ds(to, 16), :]


def solve(pieces, inverse):
    return pl.pallas_call(
        solve_kernel,
        out_shape=jax.ShapeDtypeStruct((512, 512), BF),
        in_specs=[VMEM] * 9,
        out_specs=VMEM,
        scratch_shapes=[pltpu.VMEM((512, 512), BF), pltpu.VMEM((512, 512), BF)],
        compiler_params=grant(6),
        cost_estimate=cost(270_000_000, 2_000_000),
        name="solve",
    )(*pieces, inverse)


def update_kernel(g, p0, p1, p2, p3, p4, p5, p6, p7, right, y, slab, rhs,
                  slab_out, rhs_out, wide, slab_v, rhs_v, sems):
    pieces = (p0, p1, p2, p3, p4, p5, p6, p7)
    tile = 512
    for j in range(4):
        core = jnp.concatenate([p[:, j * 256 : (j + 1) * 256] for p in pieces], axis=0)
        for i in range(2):
            rows = slice(i * tile, (i + 1) * tile)
            wide[j, rows, :] = dot(g[rows, :], core).astype(BF)
    stores = []
    for j in range(4):
        cols = slice(j * tile, (j + 1) * tile)
        change = dot_t(wide[j], right[cols, :])
        slab_v[:, cols] = (slab[:, cols].astype(F32) - change).astype(BF)
        stores.append(pltpu.make_async_copy(slab_v.at[:, cols], slab_out.at[:, cols], sems.at[j]))
        stores[-1].start()
    rhs_v[...] = (rhs[...].astype(F32) - dot(g[...], y[...])).astype(BF)
    stores.append(pltpu.make_async_copy(rhs_v, rhs_out, sems.at[4]))
    stores[-1].start()
    for copy in stores:
        copy.wait()


def update(g, pieces, right, y, slab, rhs):
    return pl.pallas_call(
        update_kernel,
        out_shape=(
            jax.ShapeDtypeStruct((1024, 2048), BF),
            jax.ShapeDtypeStruct((1024, 512), BF),
        ),
        in_specs=[VMEM] * 13,
        out_specs=(HBM, HBM),
        scratch_shapes=[
            pltpu.VMEM((4, 1024, 256), BF),
            pltpu.VMEM((1024, 2048), BF),
            pltpu.VMEM((1024, 512), BF),
            pltpu.SemaphoreType.DMA((5,)),
        ],
        compiler_params=grant(24),
        cost_estimate=cost(2_700_000_000, 12_000_000),
        name="update",
    )(g, *pieces, right, y, slab, rhs)


def per_device(
    slab,
    panel_left,
    panel_top,
    row_bases,
    col_bases,
    row_ranks,
    col_ranks,
    pivot_inverse,
    pivot_rhs,
    rhs,
):
    pack, part, bases, right = project(
        col_ranks, row_ranks, panel_left.T, row_bases, panel_top, col_bases, pivot_rhs
    )
    (inverse,) = load(pivot_inverse)
    packs = [pack] + [exchange(pack, zl=d) for d in (1, 2, 3)]
    part_far = exchange(part, zh=1)
    piece = join(packs)
    pieces = [piece] + [exchange(piece, y=d) for d in (1, 2, 3)]
    left_part = join((part, part_far))
    lefts = [left_part] + [exchange(left_part, x=d) for d in (1, 2, 3)]
    twins = [exchange(p, core=1) for p in pieces]
    y = solve(pieces + twins, inverse)
    g = left_product(lefts, bases)
    return update(g, pieces + twins, right, y, slab, rhs)


def solution(mesh):
    in_specs = (
        P("row", "col"),
        P("row", "col"),
        P("row", "col"),
        P("row", None),
        P("col", None),
        P("row"),
        P("col"),
        P(),
        P("row", "col"),
        P("row", "col"),
    )
    out_specs = (P("row", "col"), P("row", "col"))
    return jax.shard_map(
        per_device, mesh=mesh, in_specs=in_specs, out_specs=out_specs, check_vma=False
    )
```

```python
import jax
import jax.numpy as jnp
from jax import lax
from jax.experimental import pallas as pl
from jax.experimental.pallas import tpu as pltpu
from jax.sharding import PartitionSpec as P


ROW, COL = 32, 8
BF = jnp.bfloat16
F32 = jnp.float32
VMEM = pl.BlockSpec(memory_space=pltpu.VMEM)
SMEM = pl.BlockSpec(memory_space=pltpu.SMEM)
ANY = pl.BlockSpec(memory_space=pl.ANY)
HBM = pl.BlockSpec(memory_space=pltpu.HBM)


def dot(a, b):
    return lax.dot_general(a, b, (((1,), (0,)), ((), ())), preferred_element_type=F32)


def dot_t(a, b):
    return lax.dot_general(a, b, (((1,), (1,)), ((), ())), preferred_element_type=F32)


def exchange(array, zl=0, y=0, core=0, zh=0, x=0):
    row_bits = zl * 8 + y * 2 + core
    col_bits = zh * 4 + x
    pairs = [
        (r * COL + c, (r ^ row_bits) * COL + (c ^ col_bits)) for r in range(ROW) for c in range(COL)
    ]
    return lax.ppermute(array, ("row", "col"), pairs)


def grant(mib):
    return pltpu.CompilerParams(vmem_limit_bytes=mib << 20)


def cost(flops, bytes_accessed):
    return pl.CostEstimate(flops=flops, bytes_accessed=bytes_accessed, transcendentals=0)


def in_hbm(array):
    return pltpu.with_memory_space_constraint(array, pltpu.HBM)


def start_all(sources, sems):
    copies = [pltpu.make_async_copy(a, b, sems.at[n]) for n, (a, b) in enumerate(sources)]
    for copy in copies:
        copy.start()
    return copies


def project_kernel(ranks_h, rows_h, left_h, bases_h, top_h, right_h, pivot_h,
                   pack, kt, bases, right, left, top, row_ranks, ranks, sems):
    tile = 512
    sources = [(top_h, top), (ranks_h, ranks), (rows_h, row_ranks)]
    for j in range(4):
        part = slice(j * tile, (j + 1) * tile)
        sources.append((right_h.at[part], right.at[part]))
    sources.append((left_h, left))
    for i in range(2):
        part = slice(i * tile, (i + 1) * tile)
        sources.append((bases_h.at[part], bases.at[part]))
    sources.append((pivot_h, pack.at[:, 1024:]))
    for copy in start_all(sources, sems):
        copy.wait()
    lane = lax.broadcasted_iota(jnp.int32, (16, 256), 1)
    for j in range(4):
        part = dot(top[:, j * tile : (j + 1) * tile], right[j * tile : (j + 1) * tile, :])
        part = jnp.where(lane < ranks[j], part, 0.0)
        pack[:, j * 256 : (j + 1) * 256] = part.astype(BF)
    lane = lax.broadcasted_iota(jnp.int32, (64, 256), 1)
    for i in range(2):
        part = dot(left[:, i * tile : (i + 1) * tile], bases[i * tile : (i + 1) * tile, :])
        part = jnp.where(lane < row_ranks[i], part, 0.0)
        kt[:, i * 256 : (i + 1) * 256] = part.astype(BF)


def project(ranks, row_ranks, left_t, bases, top, right, pivot):
    return pl.pallas_call(
        project_kernel,
        out_shape=(
            jax.ShapeDtypeStruct((16, 1536), BF),
            jax.ShapeDtypeStruct((64, 512), BF),
            jax.ShapeDtypeStruct((1024, 256), BF),
            jax.ShapeDtypeStruct((2048, 256), BF),
        ),
        in_specs=[HBM] * 7,
        out_specs=(VMEM,) * 4,
        scratch_shapes=[
            pltpu.VMEM((64, 1024), BF),
            pltpu.VMEM((16, 2048), BF),
            pltpu.SMEM((2,), jnp.int32),
            pltpu.SMEM((4,), jnp.int32),
            pltpu.SemaphoreType.DMA((11,)),
        ],
        compiler_params=grant(8),
        cost_estimate=cost(50_000_000, 1_800_000),
        name="project",
    )(*(in_hbm(a) for a in (ranks, row_ranks, left_t, bases, top, right, pivot)))


def load_kernel(*refs):
    count = (len(refs) - 1) // 2
    copies = start_all(list(zip(refs[:count], refs[count:-1])), refs[-1])
    for copy in copies:
        copy.wait()


def load(*arrays):
    return pl.pallas_call(
        load_kernel,
        out_shape=[jax.ShapeDtypeStruct(a.shape, a.dtype) for a in arrays],
        in_specs=[HBM] * len(arrays),
        out_specs=[VMEM] * len(arrays),
        scratch_shapes=[pltpu.SemaphoreType.DMA((len(arrays),))],
        compiler_params=grant(10),
        cost_estimate=cost(0, 8_000_000),
    )(*(in_hbm(a) for a in arrays))


def join_kernel(*refs):
    out = refs[-1]
    rows = refs[0].shape[0]
    for n, piece in enumerate(refs[:-1]):
        out[n * rows : (n + 1) * rows, :] = piece[...]


def join(pieces):
    rows, columns = pieces[0].shape
    return pl.pallas_call(
        join_kernel,
        out_shape=jax.ShapeDtypeStruct((len(pieces) * rows, columns), BF),
        in_specs=[VMEM] * len(pieces),
        out_specs=VMEM,
        compiler_params=grant(4),
        cost_estimate=cost(0, 300_000),
    )(*pieces)


def place():
    r = lax.axis_index("row")
    c = lax.axis_index("col")
    return r // 8, (r // 2) % 4, r % 2, c // 4, c % 4


def blocks():
    zl, y, core, zh, x = place()
    n = 0
    for half in range(2):
        for dy in range(4):
            for dz in range(4):
                z_from, y_from, core_from = zl ^ dz, y ^ dy, core ^ half
                natural = (z_from * 4 + y_from) * 32 + core_from * 16
                col_from = z_from * 2 + y_from // 2
                turn = (col_from % 4) ^ x
                stacked = (
                    ((turn // 2) ^ ((turn % 2) * 3)) * 128
                    + ((col_from // 4) ^ zh) * 64
                    + (y_from % 2) * 32
                    + core_from * 16
                )
                yield n * 16, pl.multiple_of(natural, 16), pl.multiple_of(stacked, 16)
                n += 1


def solve_kernel(p0, p1, p2, p3, p4, p5, p6, p7, inverse, middle, ordered, natural, solved):
    pieces = (p0, p1, p2, p3, p4, p5, p6, p7)
    for at, to, _ in blocks():
        natural[pl.ds(to, 16), :] = pieces[at // 64][at % 64 : at % 64 + 16, 1024:]
    solved[...] = dot(inverse[...], natural[...]).astype(BF)
    for at, to, stacked in blocks():
        middle[pl.ds(stacked, 16), :] = pieces[at // 64][at % 64 : at % 64 + 16, :1024]
    for _, to, stacked in blocks():
        ordered[pl.ds(stacked, 16), :] = solved[pl.ds(to, 16), :]


def solve(pieces, inverse):
    return pl.pallas_call(
        solve_kernel,
        out_shape=(
            jax.ShapeDtypeStruct((512, 1024), BF),
            jax.ShapeDtypeStruct((512, 512), BF),
        ),
        in_specs=[VMEM] * 9,
        out_specs=(VMEM, VMEM),
        scratch_shapes=[pltpu.VMEM((512, 512), BF), pltpu.VMEM((512, 512), BF)],
        compiler_params=grant(8),
        cost_estimate=cost(270_000_000, 4_000_000),
        name="solve",
    )(*pieces, inverse)


def update_kernel(k0, k1, k2, k3, bases, middle, right, y, slab, rhs,
                  slab_out, rhs_out, g, wide, slab_v, rhs_v, sems):
    tile = 512
    for i in range(2):
        rows = slice(i * tile, (i + 1) * tile)
        left = jnp.concatenate([k[:, i * 256 : (i + 1) * 256] for k in (k0, k1, k2, k3)], axis=0)
        g[rows, :] = dot_t(bases[rows, :], left).astype(BF)
    for j in range(4):
        for i in range(2):
            rows = slice(i * tile, (i + 1) * tile)
            wide[j, rows, :] = dot(g[rows, :], middle[:, j * 256 : (j + 1) * 256]).astype(BF)
    stores = []
    for j in range(4):
        cols = slice(j * tile, (j + 1) * tile)
        change = dot_t(wide[j], right[cols, :])
        slab_v[:, cols] = (slab[:, cols].astype(F32) - change).astype(BF)
        stores.append(pltpu.make_async_copy(slab_v.at[:, cols], slab_out.at[:, cols], sems.at[j]))
        stores[-1].start()
    rhs_v[...] = (rhs[...].astype(F32) - dot(g[...], y[...])).astype(BF)
    stores.append(pltpu.make_async_copy(rhs_v, rhs_out, sems.at[4]))
    stores[-1].start()
    for copy in stores:
        copy.wait()


def update(lefts, bases, middle, right, y, slab, rhs):
    return pl.pallas_call(
        update_kernel,
        out_shape=(
            jax.ShapeDtypeStruct((1024, 2048), BF),
            jax.ShapeDtypeStruct((1024, 512), BF),
        ),
        in_specs=[VMEM] * 10,
        out_specs=(HBM, HBM),
        scratch_shapes=[
            pltpu.VMEM((1024, 512), BF),
            pltpu.VMEM((4, 1024, 256), BF),
            pltpu.VMEM((1024, 2048), BF),
            pltpu.VMEM((1024, 512), BF),
            pltpu.SemaphoreType.DMA((5,)),
        ],
        compiler_params=grant(26),
        cost_estimate=cost(3_000_000_000, 12_000_000),
        name="update",
    )(*lefts, bases, middle, right, y, slab, rhs)


def per_device(
    slab,
    panel_left,
    panel_top,
    row_bases,
    col_bases,
    row_ranks,
    col_ranks,
    pivot_inverse,
    pivot_rhs,
    rhs,
):
    pack, part, bases, right = project(
        col_ranks, row_ranks, panel_left.T, row_bases, panel_top, col_bases, pivot_rhs
    )
    (inverse,) = load(pivot_inverse)
    packs = [pack] + [exchange(pack, zl=d) for d in (1, 2, 3)]
    part_far = exchange(part, zh=1)
    piece = join(packs)
    pieces = [piece] + [exchange(piece, y=d) for d in (1, 2, 3)]
    left_part = join((part, part_far))
    lefts = [left_part] + [exchange(left_part, x=d) for d in (1, 2, 3)]
    twins = [exchange(p, core=1) for p in pieces]
    middle, y = solve(pieces + twins, inverse)
    lefts = [lefts[n] for n in (0, 2, 3, 1)]
    return update(lefts, bases, middle, right, y, slab, rhs)


def solution(mesh):
    in_specs = (
        P("row", "col"),
        P("row", "col"),
        P("row", "col"),
        P("row", None),
        P("col", None),
        P("row"),
        P("col"),
        P(),
        P("row", "col"),
        P("row", "col"),
    )
    out_specs = (P("row", "col"), P("row", "col"))
    return jax.shard_map(
        per_device, mesh=mesh, in_specs=in_specs, out_specs=out_specs, check_vma=False
    )
```

```python
import jax
import jax.numpy as jnp
from jax import lax
from jax.experimental import pallas as pl
from jax.experimental.pallas import tpu as pltpu
from jax.sharding import PartitionSpec as P


ROW, COL = 32, 8
BF = jnp.bfloat16
F32 = jnp.float32
VMEM = pl.BlockSpec(memory_space=pltpu.VMEM)
SMEM = pl.BlockSpec(memory_space=pltpu.SMEM)
ANY = pl.BlockSpec(memory_space=pl.ANY)
HBM = pl.BlockSpec(memory_space=pltpu.HBM)


def dot(a, b):
    return lax.dot_general(a, b, (((1,), (0,)), ((), ())), preferred_element_type=F32)


def dot_t(a, b):
    return lax.dot_general(a, b, (((1,), (1,)), ((), ())), preferred_element_type=F32)


def exchange(array, zl=0, y=0, core=0, zh=0, x=0):
    row_bits = zl * 8 + y * 2 + core
    col_bits = zh * 4 + x
    pairs = [
        (r * COL + c, (r ^ row_bits) * COL + (c ^ col_bits)) for r in range(ROW) for c in range(COL)
    ]
    return lax.ppermute(array, ("row", "col"), pairs)


def grant(mib):
    return pltpu.CompilerParams(vmem_limit_bytes=mib << 20)


def cost(flops, bytes_accessed):
    return pl.CostEstimate(flops=flops, bytes_accessed=bytes_accessed, transcendentals=0)


def in_hbm(array):
    return pltpu.with_memory_space_constraint(array, pltpu.HBM)


def start_all(sources, sems):
    copies = [pltpu.make_async_copy(a, b, sems.at[n]) for n, (a, b) in enumerate(sources)]
    for copy in copies:
        copy.start()
    return copies


def project_kernel(ranks_h, rows_h, left_h, bases_h, top_h, right_h, pivot_h,
                   pack, kt, bases, right, left, top, row_ranks, ranks, sems):
    tile = 512
    sources = [(top_h, top), (ranks_h, ranks), (rows_h, row_ranks)]
    for j in range(4):
        part = slice(j * tile, (j + 1) * tile)
        sources.append((right_h.at[part], right.at[part]))
    sources.append((left_h, left))
    for i in range(2):
        part = slice(i * tile, (i + 1) * tile)
        sources.append((bases_h.at[part], bases.at[part]))
    sources.append((pivot_h, pack.at[:, 1024:]))
    copies = start_all(sources, sems)
    for copy in copies[:7]:
        copy.wait()
    lane = lax.broadcasted_iota(jnp.int32, (16, 256), 1)
    for j in range(4):
        part = dot(top[:, j * tile : (j + 1) * tile], right[j * tile : (j + 1) * tile, :])
        part = jnp.where(lane < ranks[j], part, 0.0)
        pack[:, j * 256 : (j + 1) * 256] = part.astype(BF)
    for copy in copies[7:]:
        copy.wait()
    lane = lax.broadcasted_iota(jnp.int32, (64, 256), 1)
    for i in range(2):
        part = dot(left[:, i * tile : (i + 1) * tile], bases[i * tile : (i + 1) * tile, :])
        part = jnp.where(lane < row_ranks[i], part, 0.0)
        kt[:, i * 256 : (i + 1) * 256] = part.astype(BF)


def project(ranks, row_ranks, left_t, bases, top, right, pivot):
    return pl.pallas_call(
        project_kernel,
        out_shape=(
            jax.ShapeDtypeStruct((16, 1536), BF),
            jax.ShapeDtypeStruct((64, 512), BF),
            jax.ShapeDtypeStruct((1024, 256), BF),
            jax.ShapeDtypeStruct((2048, 256), BF),
        ),
        in_specs=[HBM] * 7,
        out_specs=(VMEM,) * 4,
        scratch_shapes=[
            pltpu.VMEM((64, 1024), BF),
            pltpu.VMEM((16, 2048), BF),
            pltpu.SMEM((2,), jnp.int32),
            pltpu.SMEM((4,), jnp.int32),
            pltpu.SemaphoreType.DMA((11,)),
        ],
        compiler_params=grant(8),
        cost_estimate=cost(50_000_000, 1_800_000),
        name="project",
    )(*(in_hbm(a) for a in (ranks, row_ranks, left_t, bases, top, right, pivot)))


def load_kernel(*refs):
    count = (len(refs) - 1) // 2
    copies = start_all(list(zip(refs[:count], refs[count:-1])), refs[-1])
    for copy in copies:
        copy.wait()


def load(*arrays):
    return pl.pallas_call(
        load_kernel,
        out_shape=[jax.ShapeDtypeStruct(a.shape, a.dtype) for a in arrays],
        in_specs=[HBM] * len(arrays),
        out_specs=[VMEM] * len(arrays),
        scratch_shapes=[pltpu.SemaphoreType.DMA((len(arrays),))],
        compiler_params=grant(10),
        cost_estimate=cost(0, 8_000_000),
    )(*(in_hbm(a) for a in arrays))


def join_kernel(*refs):
    out = refs[-1]
    rows = refs[0].shape[0]
    for n, piece in enumerate(refs[:-1]):
        out[n * rows : (n + 1) * rows, :] = piece[...]


def join(pieces):
    rows, columns = pieces[0].shape
    return pl.pallas_call(
        join_kernel,
        out_shape=jax.ShapeDtypeStruct((len(pieces) * rows, columns), BF),
        in_specs=[VMEM] * len(pieces),
        out_specs=VMEM,
        compiler_params=grant(4),
        cost_estimate=cost(0, 300_000),
    )(*pieces)


def place():
    r = lax.axis_index("row")
    c = lax.axis_index("col")
    return r // 8, (r // 2) % 4, r % 2, c // 4, c % 4


def blocks():
    zl, y, core, zh, x = place()
    n = 0
    for half in range(2):
        for dy in range(4):
            for dz in range(4):
                z_from, y_from, core_from = zl ^ dz, y ^ dy, core ^ half
                natural = (z_from * 4 + y_from) * 32 + core_from * 16
                col_from = z_from * 2 + y_from // 2
                turn = (col_from % 4) ^ x
                stacked = (
                    ((turn // 2) ^ ((turn % 2) * 3)) * 128
                    + ((col_from // 4) ^ zh) * 64
                    + (y_from % 2) * 32
                    + core_from * 16
                )
                yield n * 16, pl.multiple_of(natural, 16), pl.multiple_of(stacked, 16)
                n += 1


def solve_kernel(p0, p1, p2, p3, p4, p5, p6, p7, inverse, middle, ordered, natural, solved):
    pieces = (p0, p1, p2, p3, p4, p5, p6, p7)
    for at, to, _ in blocks():
        natural[pl.ds(to, 16), :] = pieces[at // 64][at % 64 : at % 64 + 16, 1024:]
    solved[...] = dot(inverse[...], natural[...]).astype(BF)
    for at, to, stacked in blocks():
        middle[pl.ds(stacked, 16), :] = pieces[at // 64][at % 64 : at % 64 + 16, :1024]
    for _, to, stacked in blocks():
        ordered[pl.ds(stacked, 16), :] = solved[pl.ds(to, 16), :]


def solve(pieces, inverse):
    return pl.pallas_call(
        solve_kernel,
        out_shape=(
            jax.ShapeDtypeStruct((512, 1024), BF),
            jax.ShapeDtypeStruct((512, 512), BF),
        ),
        in_specs=[VMEM] * 9,
        out_specs=(VMEM, VMEM),
        scratch_shapes=[pltpu.VMEM((512, 512), BF), pltpu.VMEM((512, 512), BF)],
        compiler_params=grant(8),
        cost_estimate=cost(270_000_000, 4_000_000),
        name="solve",
    )(*pieces, inverse)


def update_kernel(k0, k1, k2, k3, bases, middle, right, y, slab, rhs,
                  slab_out, rhs_out, g, wide, slab_v, rhs_v, sems):
    tile = 512
    for i in range(2):
        rows = slice(i * tile, (i + 1) * tile)
        left = jnp.concatenate([k[:, i * 256 : (i + 1) * 256] for k in (k0, k1, k2, k3)], axis=0)
        g[rows, :] = dot_t(bases[rows, :], left).astype(BF)
    for j in range(4):
        for i in range(2):
            rows = slice(i * tile, (i + 1) * tile)
            wide[j, rows, :] = dot(g[rows, :], middle[:, j * 256 : (j + 1) * 256]).astype(BF)
    stores = []
    for j in range(4):
        cols = slice(j * tile, (j + 1) * tile)
        change = dot_t(wide[j], right[cols, :])
        slab_v[:, cols] = (slab[:, cols].astype(F32) - change).astype(BF)
        stores.append(pltpu.make_async_copy(slab_v.at[:, cols], slab_out.at[:, cols], sems.at[j]))
        stores[-1].start()
    rhs_v[...] = (rhs[...].astype(F32) - dot(g[...], y[...])).astype(BF)
    stores.append(pltpu.make_async_copy(rhs_v, rhs_out, sems.at[4]))
    stores[-1].start()
    for copy in stores:
        copy.wait()


def update(lefts, bases, middle, right, y, slab, rhs):
    return pl.pallas_call(
        update_kernel,
        out_shape=(
            jax.ShapeDtypeStruct((1024, 2048), BF),
            jax.ShapeDtypeStruct((1024, 512), BF),
        ),
        in_specs=[VMEM] * 10,
        out_specs=(HBM, HBM),
        scratch_shapes=[
            pltpu.VMEM((1024, 512), BF),
            pltpu.VMEM((4, 1024, 256), BF),
            pltpu.VMEM((1024, 2048), BF),
            pltpu.VMEM((1024, 512), BF),
            pltpu.SemaphoreType.DMA((5,)),
        ],
        compiler_params=grant(26),
        cost_estimate=cost(3_000_000_000, 12_000_000),
        name="update",
    )(*lefts, bases, middle, right, y, slab, rhs)


def per_device(
    slab,
    panel_left,
    panel_top,
    row_bases,
    col_bases,
    row_ranks,
    col_ranks,
    pivot_inverse,
    pivot_rhs,
    rhs,
):
    pack, part, bases, right = project(
        col_ranks, row_ranks, panel_left.T, row_bases, panel_top, col_bases, pivot_rhs
    )
    (inverse,) = load(pivot_inverse)
    packs = [pack] + [exchange(pack, zl=d) for d in (1, 2, 3)]
    part_far = exchange(part, zh=1)
    piece = join(packs)
    pieces = [piece] + [exchange(piece, y=d) for d in (1, 2, 3)]
    left_part = join((part, part_far))
    lefts = [left_part] + [exchange(left_part, x=d) for d in (1, 2, 3)]
    twins = [exchange(p, core=1) for p in pieces]
    middle, y = solve(pieces + twins, inverse)
    lefts = [lefts[n] for n in (0, 2, 3, 1)]
    return update(lefts, bases, middle, right, y, slab, rhs)


def solution(mesh):
    in_specs = (
        P("row", "col"),
        P("row", "col"),
        P("row", "col"),
        P("row", None),
        P("col", None),
        P("row"),
        P("col"),
        P(),
        P("row", "col"),
        P("row", "col"),
    )
    out_specs = (P("row", "col"), P("row", "col"))
    return jax.shard_map(
        per_device, mesh=mesh, in_specs=in_specs, out_specs=out_specs, check_vma=False
    )
```

```python
import jax
import jax.numpy as jnp
from jax import lax
from jax.experimental import pallas as pl
from jax.experimental.pallas import tpu as pltpu
from jax.sharding import PartitionSpec as P


ROW, COL = 32, 8
BF = jnp.bfloat16
F32 = jnp.float32
VMEM = pl.BlockSpec(memory_space=pltpu.VMEM)
SMEM = pl.BlockSpec(memory_space=pltpu.SMEM)
ANY = pl.BlockSpec(memory_space=pl.ANY)
HBM = pl.BlockSpec(memory_space=pltpu.HBM)


def dot(a, b):
    return lax.dot_general(a, b, (((1,), (0,)), ((), ())), preferred_element_type=F32)


def dot_t(a, b):
    return lax.dot_general(a, b, (((1,), (1,)), ((), ())), preferred_element_type=F32)


def exchange(array, zl=0, y=0, core=0, zh=0, x=0):
    row_bits = zl * 8 + y * 2 + core
    col_bits = zh * 4 + x
    pairs = [
        (r * COL + c, (r ^ row_bits) * COL + (c ^ col_bits)) for r in range(ROW) for c in range(COL)
    ]
    return lax.ppermute(array, ("row", "col"), pairs)


def grant(mib):
    return pltpu.CompilerParams(vmem_limit_bytes=mib << 20)


def cost(flops, bytes_accessed):
    return pl.CostEstimate(flops=flops, bytes_accessed=bytes_accessed, transcendentals=0)


def in_hbm(array):
    return pltpu.with_memory_space_constraint(array, pltpu.HBM)


def start_all(sources, sems):
    copies = [pltpu.make_async_copy(a, b, sems.at[n]) for n, (a, b) in enumerate(sources)]
    for copy in copies:
        copy.start()
    return copies


def project_kernel(ranks_h, rows_h, left_h, bases_h, top_h, right_h, pivot_h,
                   pack, kt, bases, right, left, top, row_ranks, ranks, sems):
    tile = 512
    sources = [(top_h, top), (ranks_h, ranks), (rows_h, row_ranks)]
    for j in range(4):
        part = slice(j * tile, (j + 1) * tile)
        sources.append((right_h.at[part], right.at[part]))
    sources.append((left_h, left))
    for i in range(2):
        part = slice(i * tile, (i + 1) * tile)
        sources.append((bases_h.at[part], bases.at[part]))
    sources.append((pivot_h, pack.at[:, 1024:]))
    copies = start_all(sources, sems)
    for copy in copies[:7]:
        copy.wait()
    lane = lax.broadcasted_iota(jnp.int32, (16, 256), 1)
    for j in range(4):
        part = dot(top[:, j * tile : (j + 1) * tile], right[j * tile : (j + 1) * tile, :])
        part = jnp.where(lane < ranks[j], part, 0.0)
        pack[:, j * 256 : (j + 1) * 256] = part.astype(BF)
    for copy in copies[7:]:
        copy.wait()
    lane = lax.broadcasted_iota(jnp.int32, (64, 256), 1)
    for i in range(2):
        part = dot(left[:, i * tile : (i + 1) * tile], bases[i * tile : (i + 1) * tile, :])
        part = jnp.where(lane < row_ranks[i], part, 0.0)
        kt[:, i * 256 : (i + 1) * 256] = part.astype(BF)


def project(ranks, row_ranks, left_t, bases, top, right, pivot):
    return pl.pallas_call(
        project_kernel,
        out_shape=(
            jax.ShapeDtypeStruct((16, 1536), BF),
            jax.ShapeDtypeStruct((64, 512), BF),
            jax.ShapeDtypeStruct((1024, 256), BF),
            jax.ShapeDtypeStruct((2048, 256), BF),
        ),
        in_specs=[HBM] * 7,
        out_specs=(VMEM,) * 4,
        scratch_shapes=[
            pltpu.VMEM((64, 1024), BF),
            pltpu.VMEM((16, 2048), BF),
            pltpu.SMEM((2,), jnp.int32),
            pltpu.SMEM((4,), jnp.int32),
            pltpu.SemaphoreType.DMA((11,)),
        ],
        compiler_params=grant(8),
        cost_estimate=cost(50_000_000, 1_800_000),
        name="project",
    )(*(in_hbm(a) for a in (ranks, row_ranks, left_t, bases, top, right, pivot)))


def load_kernel(*refs):
    count = (len(refs) - 1) // 2
    copies = start_all(list(zip(refs[:count], refs[count:-1])), refs[-1])
    for copy in copies:
        copy.wait()


def load(*arrays):
    return pl.pallas_call(
        load_kernel,
        out_shape=[jax.ShapeDtypeStruct(a.shape, a.dtype) for a in arrays],
        in_specs=[HBM] * len(arrays),
        out_specs=[VMEM] * len(arrays),
        scratch_shapes=[pltpu.SemaphoreType.DMA((len(arrays),))],
        compiler_params=grant(10),
        cost_estimate=cost(0, 8_000_000),
    )(*(in_hbm(a) for a in arrays))


def join_kernel(*refs):
    out = refs[-1]
    rows = refs[0].shape[0]
    for n, piece in enumerate(refs[:-1]):
        out[n * rows : (n + 1) * rows, :] = piece[...]


def join(pieces):
    rows, columns = pieces[0].shape
    return pl.pallas_call(
        join_kernel,
        out_shape=jax.ShapeDtypeStruct((len(pieces) * rows, columns), BF),
        in_specs=[VMEM] * len(pieces),
        out_specs=VMEM,
        compiler_params=grant(4),
        cost_estimate=cost(0, 300_000),
    )(*pieces)


def place():
    r = lax.axis_index("row")
    c = lax.axis_index("col")
    return r // 8, (r // 2) % 4, r % 2, c // 4, c % 4


def blocks():
    zl, y, core, zh, x = place()
    n = 0
    for half in range(2):
        for dy in range(4):
            for dz in range(4):
                z_from, y_from, core_from = zl ^ dz, y ^ dy, core ^ half
                natural = (z_from * 4 + y_from) * 32 + core_from * 16
                col_from = z_from * 2 + y_from // 2
                turn = (col_from % 4) ^ x
                stacked = (
                    ((turn // 2) ^ ((turn % 2) * 3)) * 128
                    + ((col_from // 4) ^ zh) * 64
                    + (y_from % 2) * 32
                    + core_from * 16
                )
                yield n * 16, pl.multiple_of(natural, 16), pl.multiple_of(stacked, 16)
                n += 1


def solve_kernel(p0, p1, p2, p3, p4, p5, p6, p7, inverse, middle, ordered, natural, solved):
    pieces = (p0, p1, p2, p3, p4, p5, p6, p7)
    for at, to, _ in blocks():
        natural[pl.ds(to, 16), :] = pieces[at // 64][at % 64 : at % 64 + 16, 1024:]
    solved[...] = dot(inverse[...], natural[...]).astype(BF)
    for at, to, stacked in blocks():
        middle[pl.ds(stacked, 16), :] = pieces[at // 64][at % 64 : at % 64 + 16, :1024]
    for _, to, stacked in blocks():
        ordered[pl.ds(stacked, 16), :] = solved[pl.ds(to, 16), :]


def solve(pieces, inverse):
    return pl.pallas_call(
        solve_kernel,
        out_shape=(
            jax.ShapeDtypeStruct((512, 1024), BF),
            jax.ShapeDtypeStruct((512, 512), BF),
        ),
        in_specs=[VMEM] * 9,
        out_specs=(VMEM, VMEM),
        scratch_shapes=[pltpu.VMEM((512, 512), BF), pltpu.VMEM((512, 512), BF)],
        compiler_params=grant(8),
        cost_estimate=cost(270_000_000, 4_000_000),
        name="solve",
    )(*pieces, inverse)


def update_kernel(k0, k1, k2, k3, bases, middle, right, y, slab, rhs,
                  slab_out, rhs_out, g, wide, slab_v, rhs_v, sems):
    tile = 512
    for i in range(2):
        rows = slice(i * tile, (i + 1) * tile)
        left = jnp.concatenate([k[:, i * 256 : (i + 1) * 256] for k in (k0, k1, k2, k3)], axis=0)
        g[rows, :] = dot_t(bases[rows, :], left).astype(BF)
    for j in range(4):
        for i in range(2):
            rows = slice(i * tile, (i + 1) * tile)
            wide[j, rows, :] = dot(g[rows, :], middle[:, j * 256 : (j + 1) * 256]).astype(BF)
    stores = []
    for j in range(4):
        cols = slice(j * tile, (j + 1) * tile)
        change = dot_t(wide[j], right[cols, :])
        slab_v[:, cols] = (slab[:, cols].astype(F32) - change).astype(BF)
        stores.append(pltpu.make_async_copy(slab_v.at[:, cols], slab_out.at[:, cols], sems.at[j]))
        stores[-1].start()
    for i in range(2):
        rows = slice(i * tile, (i + 1) * tile)
        rhs_v[rows, :] = (rhs[rows, :].astype(F32) - dot(g[rows, :], y[...])).astype(BF)
        stores.append(pltpu.make_async_copy(rhs_v.at[rows], rhs_out.at[rows], sems.at[4 + i]))
        stores[-1].start()
    for copy in stores:
        copy.wait()


def update(lefts, bases, middle, right, y, slab, rhs):
    return pl.pallas_call(
        update_kernel,
        out_shape=(
            jax.ShapeDtypeStruct((1024, 2048), BF),
            jax.ShapeDtypeStruct((1024, 512), BF),
        ),
        in_specs=[VMEM] * 10,
        out_specs=(HBM, HBM),
        scratch_shapes=[
            pltpu.VMEM((1024, 512), BF),
            pltpu.VMEM((4, 1024, 256), BF),
            pltpu.VMEM((1024, 2048), BF),
            pltpu.VMEM((1024, 512), BF),
            pltpu.SemaphoreType.DMA((6,)),
        ],
        compiler_params=grant(26),
        cost_estimate=cost(3_000_000_000, 12_000_000),
        name="update",
    )(*lefts, bases, middle, right, y, slab, rhs)


def per_device(
    slab,
    panel_left,
    panel_top,
    row_bases,
    col_bases,
    row_ranks,
    col_ranks,
    pivot_inverse,
    pivot_rhs,
    rhs,
):
    pack, part, bases, right = project(
        col_ranks, row_ranks, panel_left.T, row_bases, panel_top, col_bases, pivot_rhs
    )
    (inverse,) = load(pivot_inverse)
    packs = [pack] + [exchange(pack, zl=d) for d in (1, 2, 3)]
    part_far = exchange(part, zh=1)
    piece = join(packs)
    pieces = [piece] + [exchange(piece, y=d) for d in (1, 2, 3)]
    left_part = join((part, part_far))
    lefts = [left_part] + [exchange(left_part, x=d) for d in (1, 2, 3)]
    twins = [exchange(p, core=1) for p in pieces]
    middle, y = solve(pieces + twins, inverse)
    lefts = [lefts[n] for n in (0, 2, 3, 1)]
    return update(lefts, bases, middle, right, y, slab, rhs)


def solution(mesh):
    in_specs = (
        P("row", "col"),
        P("row", "col"),
        P("row", "col"),
        P("row", None),
        P("col", None),
        P("row"),
        P("col"),
        P(),
        P("row", "col"),
        P("row", "col"),
    )
    out_specs = (P("row", "col"), P("row", "col"))
    return jax.shard_map(
        per_device, mesh=mesh, in_specs=in_specs, out_specs=out_specs, check_vma=False
    )
```
